32 devices in a mesh: slab: 32 (over z, y, x, core).
Axes of the slice: x: 2, y: 2, z: 4, core: 2. Of those that a mesh axis runs over, the one named last changes fastest.
Arguments:
- tensor: float32 [128, 1024, 512], P('slab'), may hold values from 0 to 1024
- first: float32 [128, 512], P('slab'), may hold values from 0.01 to 2.01
- second: float32 [1024, 512], replicated, may hold values from 0.01 to 2.01
- third: float32 [512, 512], replicated, may hold values from 0.01 to 2.01
Outputs:
- new_first: float32 [128, 512], P('slab')
- new_second: float32 [1024, 512], P('slab')
- new_third: float32 [512, 512], P('slab')
The draws below stay inside these ranges and needn't reach their ends.
All inputs are finite; a program needn't handle non-finite values.
Results may differ from the reference program's by a relative error of at most 0.0002.
Values sent between devices are 32-bit elements; how exact they have to be, the bound alone decides.
No kernel may reach another device: no remote copies, remote signals or barrier semaphores. Data moves between devices by JAX's collectives and lax.ppermute only.
A program may use at most 64 MiB of HBM per device.

```python
import math
import jax
import jax.numpy as jnp
from jax import lax

J = 1024
K = 512
R = 512
I = 128


signal_rank = 64


signal_scale = 14.0


upper_bound = 1024.0


def sparse_factor(key, row_count, col_count):
    key_mask = jax.random.fold_in(key, 101)
    key_value = jax.random.fold_in(key, 202)
    fraction = 0.125
    magnitude = 2.0 * jax.random.uniform(key_value, (row_count, col_count), jnp.float32)
    keep_mask = (jax.random.uniform(key_mask, (row_count, col_count), jnp.float32) < fraction).astype(jnp.float32)
    return 0.01 + keep_mask * magnitude


def draw_tensor(key, part):
    left_factor = sparse_factor(jax.random.fold_in(key, 11), I, signal_rank)
    middle_factor = sparse_factor(jax.random.fold_in(key, 12), J, signal_rank)
    right_factor = sparse_factor(jax.random.fold_in(key, 13), K, signal_rank)
    paired = (left_factor[:, None, :] * middle_factor[None, :, :]).reshape(I * J, signal_rank)
    signal = jnp.dot(paired, right_factor.T, precision=lax.Precision.HIGHEST).reshape(I, J, K)
    noise_part = jax.random.uniform(jax.random.fold_in(key, 14), (I, J, K), jnp.float32)
    return jnp.minimum(signal_scale * signal + noise_part, upper_bound)


def draw_first(key, part):
    return sparse_factor(jax.random.fold_in(key, 21), I, R)


def draw_second(key, part):
    return sparse_factor(jax.random.fold_in(key, 22), J, R)


def draw_third(key, part):
    return sparse_factor(jax.random.fold_in(key, 23), K, R)


def setup_inputs(seed: int = 0) -> dict:
    key_of = jax.random.split(jax.random.key(seed), 5)
    tensor = draw_tensor(jax.random.fold_in(key_of[4], 71), 0)
    first = draw_first(jax.random.fold_in(key_of[4], 71), 0)
    second = draw_second(jax.random.fold_in(key_of[4], 71), 0)
    third = draw_third(jax.random.fold_in(key_of[4], 71), 0)
    return {"tensor": tensor, "first": first, "second": second, "third": third}


def update(start_rows, sums, gram):
    highest = lax.Precision.HIGHEST
    lipschitz = jnp.max(jnp.sum(gram, axis=1))
    previous = start_rows
    extrapolated = start_rows
    updated = start_rows
    for turn in range(4):
        gradient = jnp.dot(extrapolated, gram, precision=highest) - sums
        updated = jnp.maximum(extrapolated - gradient / lipschitz, 0.0)
        extrapolated = updated + (turn / (turn + 3.0)) * (updated - previous)
        previous = updated
    return updated


def reference(tensor, first, second, third):
    highest = lax.Precision.HIGHEST
    rows_block = math.gcd(I, 32)
    blocks_count = I // rows_block
    slab_blocks = tensor.reshape(blocks_count, rows_block, J, K)
    gram_second = jnp.dot(second.T, second, precision=highest)
    gram_third = jnp.dot(third.T, third, precision=highest)

    def mode_one(slab_block):
        partial_value = jnp.einsum('ijk,kr->ijr', slab_block, third, precision=highest)
        return jnp.einsum('ijr,jr->ir', partial_value, second, precision=highest)

    first_sums = lax.map(mode_one, slab_blocks).reshape(I, R)
    new_first = update(first, first_sums, gram_second * gram_third)
    gram_first = jnp.dot(new_first.T, new_first, precision=highest)
    first_blocks = new_first.reshape(blocks_count, rows_block, R)

    def mode_two(totals, paired):
        slab_block, own_rows = paired
        partial_value = jnp.einsum('ijk,kr->ijr', slab_block, third, precision=highest)
        return totals + jnp.einsum('ijr,ir->jr', partial_value, own_rows, precision=highest), None

    second_sums, _ = lax.scan(mode_two, jnp.zeros((J, R), jnp.float32), (slab_blocks, first_blocks))
    new_second = update(second, second_sums, gram_first * gram_third)
    gram_new_second = jnp.dot(new_second.T, new_second, precision=highest)

    def mode_three(totals, paired):
        slab_block, own_rows = paired
        weighted = new_second[None, :, :] * own_rows[:, None, :]
        return totals + jnp.einsum('ijk,ijr->kr', slab_block, weighted, precision=highest), None

    third_sums, _ = lax.scan(mode_three, jnp.zeros((K, R), jnp.float32), (slab_blocks, first_blocks))
    new_third = update(third, third_sums, gram_first * gram_new_second)
    return (new_first, new_second, new_third)
```

```python
import jax
import jax.numpy as jnp
from jax import lax
from jax.sharding import PartitionSpec as P

AXIS = "slab"
PREC = lax.Precision.HIGH


def update(start_rows, sums, gram):
    inverse = 1.0 / jnp.max(jnp.sum(gram, axis=1))
    previous = start_rows
    extrapolated = start_rows
    updated = start_rows
    for turn in range(4):
        gradient = jnp.dot(extrapolated, gram, precision=PREC) - sums
        updated = jnp.maximum(extrapolated - gradient * inverse, 0.0)
        extrapolated = updated + turn / (turn + 3.0) * (updated - previous)
        previous = updated
    return updated


def swap(value, devices_count, mask):
    return lax.ppermute(value, AXIS, [(i, i ^ mask) for i in range(devices_count)])


def pick(value, axis, index):
    return lax.dynamic_index_in_dim(value, index, axis, keepdims=False)


def my_bits(index, bits):
    number = 0
    for place, bit in enumerate(bits):
        number = number + (((index >> bit) & 1) << place)
    return number


def groups_of(bits_count):
    rest = list(range(min(3, bits_count), bits_count))
    return [tuple(rest[i : i + 2]) for i in range(0, len(rest), 2)]


def spread(number, bits):
    return sum(((number >> place) & 1) << bit for place, bit in enumerate(bits))


def scatter_bit(blocks, bits, bit, index, devices_count):
    place = bits.index(bit)
    shape = blocks.shape
    split = blocks.reshape(shape[0] >> (place + 1), 2, 1 << place, *shape[1:])
    mine = (index >> bit) & 1
    away = pick(split, 1, 1 - mine)
    kept = pick(split, 1, mine)
    came = swap(away, devices_count, 1 << bit)
    total = (kept + came).reshape(shape[0] // 2, *shape[1:])
    return total, [b for b in bits if b != bit]


def reduce_scatter(blocks, index, devices_count):
    bits = list(range(devices_count.bit_length() - 1))
    all_bits = len(bits)
    if 0 in bits:
        blocks, bits = scatter_bit(blocks, bits, 0, index, devices_count)
    half = blocks.shape[-1] // 2
    lanes = [blocks[..., :half], blocks[..., half:]]
    orders = [[b for b in (1, 2) if b in bits], [b for b in (2, 1) if b in bits]]
    left = bits
    for lane in range(2):
        left = bits
        for bit in orders[lane]:
            lanes[lane], left = scatter_bit(lanes[lane], left, bit, index, devices_count)
    blocks = jnp.concatenate(lanes, axis=-1)
    bits = left
    for group in groups_of(all_bits):
        size = 1 << len(group)
        split = blocks.reshape(blocks.shape[0] // size, size, *blocks.shape[1:])
        mine = my_bits(index, group)
        total = pick(split, 1, mine)
        for turn in range(1, size):
            away = pick(split, 1, mine ^ turn)
            total = total + swap(away, devices_count, spread(turn, group))
        blocks = total
        bits = [b for b in bits if b not in group]
    return blocks[0]


def gather_bits(blocks, bits, group, index, devices_count):
    size = 1 << len(group)
    pieces = [blocks] + [
        swap(blocks, devices_count, spread(turn, group)) for turn in range(1, size)
    ]
    mine = my_bits(index, group)
    stacked = jnp.stack(pieces)
    order = jnp.stack([pick(stacked, 0, mine ^ place) for place in range(size)], axis=1)
    return order.reshape(blocks.shape[0] * size, *blocks.shape[1:]), list(group) + bits


def all_gather(block, index, devices_count):
    bits_count = devices_count.bit_length() - 1
    blocks = block[None]
    bits = []
    for group in reversed(groups_of(bits_count)):
        blocks, bits = gather_bits(blocks, bits, group, index, devices_count)
    half = blocks.shape[-1] // 2
    lanes = [blocks[..., :half], blocks[..., half:]]
    low = [b for b in (2, 1) if b < bits_count]
    for lane in range(2):
        order = low if lane == 0 else low[::-1]
        for bit in order:
            lanes[lane], _ = gather_bits(lanes[lane], [], (bit,), index, devices_count)
    if len(low) == 2:
        shape = lanes[1].shape
        lanes[1] = (
            lanes[1].reshape(shape[0] // 4, 2, 2, *shape[1:]).swapaxes(1, 2).reshape(shape)
        )
    blocks = jnp.concatenate(lanes, axis=-1)
    if bits_count:
        blocks, bits = gather_bits(blocks, [], (0,), index, devices_count)
    return blocks.reshape(-1, block.shape[-1])


def gather_rows(rows, devices_count):
    bits_count = devices_count.bit_length() - 1
    for group in groups_of(bits_count)[::-1] + [(b,) for b in (2, 1, 0) if b < bits_count]:
        pieces = [rows] + [
            swap(rows, devices_count, spread(turn, group)) for turn in range(1, 1 << len(group))
        ]
        rows = jnp.concatenate(pieces, axis=0)
    return rows


def body(tensor, first, second, third):
    devices_count = lax.axis_size(AXIS)
    index = lax.axis_index(AXIS)
    slabs = tensor.shape[0]
    rank = third.shape[1]
    second_count = second.shape[0] // devices_count
    third_count = third.shape[0] // devices_count
    gram_second = jnp.dot(second.T, second, precision=PREC)
    gram_third = jnp.dot(third.T, third, precision=PREC)
    partial_value = jnp.einsum("ijk,kr->ijr", tensor, third, precision=PREC)
    first_sums = jnp.sum(partial_value * second[None], axis=1)
    new_first = update(first, first_sums, gram_second * gram_third)
    every_first = gather_rows(new_first, devices_count)
    gram_first = jnp.dot(every_first.T, every_first, precision=PREC)
    own_term = jnp.sum(partial_value * new_first[:, None, :], axis=0)
    second_rows = reduce_scatter(
        own_term.reshape(devices_count, second_count, rank), index, devices_count
    )
    own_second = lax.dynamic_slice_in_dim(second, index * second_count, second_count, 0)
    out_second = update(own_second, second_rows, gram_first * gram_third)
    whole_second = all_gather(out_second, index, devices_count)
    third_sums = 0.0
    for slab in range(slabs):
        product = lax.dot_general(
            tensor[slab], whole_second, (((0,), (0,)), ((), ())), precision=PREC
        )
        third_sums = third_sums + product * new_first[slab][None, :]
    gram_new_second = jnp.dot(whole_second.T, whole_second, precision=PREC)
    third_rows = reduce_scatter(
        third_sums.reshape(devices_count, third_count, rank), index, devices_count
    )
    own_third = lax.dynamic_slice_in_dim(third, index * third_count, third_count, 0)
    new_third = update(own_third, third_rows, gram_first * gram_new_second)
    return (new_first, out_second, new_third)


def solution(mesh):
    in_specs = (P(AXIS, None, None), P(AXIS, None), P(), P())
    out_specs = (P(AXIS, None), P(AXIS, None), P(AXIS, None))
    return jax.shard_map(body, mesh=mesh, in_specs=in_specs, out_specs=out_specs, check_vma=False)
```
